32 devices in a mesh: groups: 2 (over y), ctx: 8 (over z, x), chan: 2 (over core).
Axes of the slice: x: 2, y: 2, z: 4, core: 2. Of those that a mesh axis runs over, the one named last changes fastest.
Arguments:
- inputs: bfloat16 [2048, 2048], P(('groups', 'ctx'), 'chan'), parts along dimension 0, may hold values from -0.1875 to 0.1875
- out_grad: bfloat16 [2048, 2048], P(('groups', 'ctx'), 'chan'), parts along dimension 0, may hold values from -6 to 6
- filters: bfloat16 [512, 2048], P(None, 'chan'), may hold values from -0.25 to 0.25
Outputs:
- in_grad: bfloat16 [2048, 2048], P(('groups', 'ctx'), 'chan'), parts along dimension 0
- filter_grad: float32 [1024, 2048], P(('groups', 'ctx'), 'chan'), parts along dimension 0
The draws below stay inside these ranges and needn't reach their ends.
There are 2 independent parts, one for each index of `groups`. The reference program is written for one: setup_inputs(seed, part) draws one part's arguments, and reference() takes and returns one part's arrays. A program takes and returns all parts, laid end to end along the dimension named above; an argument that names none is the same for every part. Nothing has to cross between parts.
All inputs are finite; a program needn't handle non-finite values.
Results may differ from the reference program's by a relative error of at most 0.0085.
Values may be sent and summed in bfloat16 or wider, within the bound.
A program may use at most 64 MiB of HBM per device.

```python
import jax
import jax.numpy as jnp

CH = 2048
LAGS = 512
SEQ = 1024


def steps_of(rng, dims, split, low, top_value):
    factor_of = 1.0
    for position, parts in split:
        draws = jax.random.uniform(jax.random.fold_in(jax.random.fold_in(rng, 6), position), (parts,), jnp.float32, low / len(split), top_value / len(split))
        factor_of = factor_of * jnp.repeat(jnp.exp(draws), dims[position] // parts).reshape((-1,) + (1,) * (len(dims) - 1 - position))
    return factor_of


def scatter_about(stream_key, extent, deviation, bound, shards=(), held_as=jnp.bfloat16):
    loudness = steps_of(stream_key, extent, shards, -0.22, 0.18) if shards else 1.0
    array = jax.random.normal(stream_key, extent, jnp.float32) * deviation * loudness
    return jnp.minimum(jnp.maximum(array, -bound), bound).astype(held_as)


def setup_inputs(seed: int = 0, part: int = 0) -> dict:
    key_of = jax.random.split(jax.random.key(seed), 4)
    own_keys = jax.random.split(jax.random.fold_in(key_of[3], part), 4)
    inputs = scatter_about(own_keys[0], (SEQ, CH), SEQ ** -0.5, 0.1875, ((0, 8), (1, 2)))
    out_grad = scatter_about(own_keys[1], (SEQ, CH), 1.0, 6.0, ((0, 8), (1, 2)))
    filters = scatter_about(key_of[2], (LAGS, CH), LAGS ** -0.5, 0.25, ((1, 2),))
    return dict(inputs=inputs, out_grad=out_grad, filters=filters)


def reference(inputs, out_grad, filters):
    positions = inputs.shape[0]
    period = 2 * positions
    values = inputs.astype(jnp.float32)
    grads = out_grad.astype(jnp.float32)
    taps = filters.astype(jnp.float32)
    spec_in = jnp.fft.rfft(values, n=period, axis=0)
    spec_grad = jnp.fft.rfft(grads, n=period, axis=0)
    spec_taps = jnp.fft.rfft(taps, n=period, axis=0)
    in_grad = jnp.fft.irfft(jnp.conj(spec_taps) * spec_grad, n=period, axis=0)[:positions]
    filter_grad = jnp.fft.irfft(spec_grad * jnp.conj(spec_in), n=period, axis=0)[:filters.shape[0]]
    return in_grad.astype(jnp.bfloat16), filter_grad.astype(jnp.float32)
```

```python
import functools
import math

import jax
import jax.numpy as jnp
import numpy as np
from jax import lax
from jax.experimental import pallas as pl
from jax.experimental.pallas import tpu as pltpu
from jax.sharding import PartitionSpec as P

LANES = 128
CHUNK = 16
CHUNKS = 2


def passed_along(value, axis, steps):
    count = lax.axis_size(axis)
    initial, last = (max(0, -steps), min(count, count - steps))
    return lax.ppermute(value, axis, [(source, source + steps) for source in range(initial, last)])


def phase_table(row_ids, col_ids, period):
    return 2.0 * math.pi / period * (row_ids * col_ids % period).astype(jnp.float32)


def split_table(table):
    high_part = table.astype(jnp.bfloat16)
    low_part = (table - high_part.astype(jnp.float32)).astype(jnp.bfloat16)
    return (high_part, low_part)


def forward_apply(parts, data):
    first = jnp.dot(parts[0], data, preferred_element_type=jnp.float32)
    return first + jnp.dot(parts[1], data, preferred_element_type=jnp.float32)


def spectral(table, data):
    return jnp.dot(table, data, precision=lax.Precision.HIGH, preferred_element_type=jnp.float32)


def general_plan(inputs, out_grad, filters):
    tok_len = out_grad.shape[0]
    channels = out_grad.shape[1]
    lag_count = filters.shape[0]
    far_reach = lag_count // tok_len
    period = 2 * tok_len
    freq_count = tok_len + 1
    freq_col = jnp.arange(freq_count, dtype=jnp.int32)[:, None]
    time_row = jnp.arange(tok_len, dtype=jnp.int32)[None, :]
    angle_fwd = phase_table(freq_col, time_row, period)
    forward = split_table(jnp.concatenate([jnp.cos(angle_fwd), -jnp.sin(angle_fwd)], axis=0))
    freq_row = jnp.arange(freq_count, dtype=jnp.int32)[None, :]
    weighting = (
        jnp.where((freq_row == 0) | (freq_row == tok_len), 1.0, 2.0).astype(jnp.float32) / period
    )
    back_rows = (tok_len - jnp.arange(tok_len, dtype=jnp.int32))[:, None]
    angle_back = phase_table(back_rows, freq_row, period)
    inverse_in = jnp.concatenate(
        [weighting * jnp.cos(angle_back), -weighting * jnp.sin(angle_back)], axis=1
    )
    lag_rows = ((jnp.arange(period, dtype=jnp.int32) - tok_len) % period)[:, None]
    angle_lag = phase_table(lag_rows, freq_row, period)
    inverse_lag = jnp.concatenate(
        [weighting * jnp.cos(angle_lag), -weighting * jnp.sin(angle_lag)], axis=1
    )
    parity = jnp.where(jnp.arange(freq_count) % 2 == 0, 1.0, -1.0).astype(jnp.float32)
    parity_both = jnp.concatenate([parity, parity])[:, None]
    received = [out_grad]
    current = out_grad
    for offset in range(far_reach):
        current = passed_along(current, "ctx", -1)
        received.append(current)
    tap_blocks = filters.reshape(far_reach, tok_len, channels)
    tap_spec = jnp.einsum("ft,btc->bfc", forward[0], tap_blocks, preferred_element_type=jnp.float32)
    tap_spec = tap_spec + jnp.einsum(
        "ft,btc->bfc", forward[1], tap_blocks, preferred_element_type=jnp.float32
    )
    input_spec = forward_apply(forward, inputs)
    input_re = input_spec[:freq_count]
    input_im = input_spec[freq_count:]
    accum_re = jnp.zeros((freq_count, channels), jnp.float32)
    accum_im = jnp.zeros((freq_count, channels), jnp.float32)
    lag_parts = []
    for offset in range(far_reach + 1):
        grad_spec = forward_apply(forward, received[offset])
        grad_re = grad_spec[:freq_count]
        grad_im = grad_spec[freq_count:]
        if offset >= 1 and offset < far_reach:
            segment = tap_spec[offset - 1] + parity_both * tap_spec[offset]
        elif offset >= 1:
            segment = tap_spec[offset - 1]
        else:
            segment = parity_both * tap_spec[offset]
        seg_re = segment[:freq_count]
        seg_im = segment[freq_count:]
        accum_re = accum_re + grad_re * seg_re + grad_im * seg_im
        accum_im = accum_im + grad_re * seg_im - grad_im * seg_re
        cross = jnp.concatenate(
            [grad_re * input_re + grad_im * input_im, grad_im * input_re - grad_re * input_im],
            axis=0,
        )
        lag_parts.append(spectral(inverse_lag, cross))
    in_grad = spectral(inverse_in, jnp.concatenate([accum_re, accum_im], axis=0)).astype(
        jnp.bfloat16
    )
    segments = [
        lag_parts[index + 1][:tok_len] + lag_parts[index][tok_len:] for index in range(far_reach)
    ]
    partial_value = jnp.concatenate(segments, axis=0)
    filter_grad = lax.psum_scatter(partial_value, "ctx", scatter_dimension=0, tiled=True)
    return (in_grad, filter_grad)


def table_parts(table):
    high_part = table.astype(jnp.bfloat16)
    low_part = (table - high_part.astype(np.float64)).astype(jnp.bfloat16)
    return np.stack([high_part, low_part])


def transform_tables(block):
    order = np.concatenate([np.arange(0, block, 2), np.arange(1, block, 2)])
    steps = (2 * order + 1)[:, None] * np.arange(block)[None, :] % (4 * block)
    angle = np.pi / (2 * block) * steps
    forward = np.concatenate([np.cos(angle), np.sin(angle)], axis=0)
    return table_parts(forward), table_parts(forward.T / block)


def wait_for(like, sem):
    pltpu.make_async_copy(like, like, sem).wait()


def chain_kernel(
    pair, block, chunks,
    in_ref, grad_ref, taps_ref, fwd_hbm, inv_hbm,
    out_ref, lag_ref,
    g_buf, u_buf, tap_buf, fwd, inv, g_spec, u_spec, tap_spec, r_high, r_low, in_buf, part, own_low, next_low,
    gx_sem, ux_sem, direct_sem, passed_sem, far_sem, left_u_sem, low_sem, lag_sem, out_sem, send_sem, local_sem,
    ready, ready_far,
):
    me = lax.axis_index("ctx")
    level = lax.div(me, pair)
    side = lax.rem(me, pair)
    mate = me + 1 - 2 * side
    left, right = me - pair, me + pair
    tok_len, channels = in_ref.shape
    lag_count = taps_ref.shape[0]
    width = g_buf.shape[3]
    half = chunks * width
    segs = lag_count // block
    levels = 2 * segs
    own_lags = lag_count // (levels * pair)

    def cols(which, c):
        return pl.ds(pl.multiple_of(which * half + c * width, LANES), width)

    def rows(which, length):
        return pl.ds(pl.multiple_of(which * length, length), length)

    mine, other = rows(side, tok_len), rows(1 - side, tok_len)

    def remote(source, target, send, recv, device):
        pltpu.make_async_remote_copy(
            src_ref=source, dst_ref=target, send_sem=send, recv_sem=recv,
            device_id={"ctx": device}, device_id_type=pl.DeviceIdType.MESH,
        ).start()

    def signal(sem, device):
        pl.semaphore_signal(
            sem, inc=1, device_id={"ctx": device}, device_id_type=pl.DeviceIdType.MESH
        )

    def at_level(*which):
        hit = level == which[0]
        for value in which[1:]:
            hit = jnp.logical_or(hit, level == value)
        return pl.when(hit)

    barrier = pltpu.get_barrier_semaphore()
    signal(barrier, mate)

    @pl.when(level < levels - 1)
    def _():
        signal(barrier, right)

    pltpu.make_async_copy(taps_ref.at[:, rows_of_half(side, half)], tap_buf, local_sem.at[1]).start()
    pltpu.make_async_copy(fwd_hbm, fwd, local_sem.at[0]).start()
    for c in range(chunks):
        pltpu.make_async_copy(grad_ref.at[:, cols(side, c)], g_buf.at[0, c, mine, :], gx_sem.at[c]).start()
    for c in range(chunks):
        pltpu.make_async_copy(in_ref.at[:, cols(side, c)], u_buf.at[0, c, mine, :], ux_sem.at[c]).start()
    pltpu.make_async_copy(inv_hbm, inv, local_sem.at[2]).start()

    pl.semaphore_wait(barrier, 1 + jnp.minimum(level, 1))

    @pl.when(level > 0)
    def _():
        for c in range(chunks):
            remote(grad_ref.at[:, cols(side, c)], g_buf.at[1, c, mine, :], send_sem.at[1], direct_sem.at[c], left)

    for c in range(chunks):
        remote(grad_ref.at[:, cols(1 - side, c)], g_buf.at[0, c, mine, :], send_sem.at[0], gx_sem.at[c], mate)
    for c in range(chunks):
        remote(in_ref.at[:, cols(1 - side, c)], u_buf.at[0, c, mine, :], send_sem.at[0], ux_sem.at[c], mate)

    @at_level(1)
    def _():
        signal(ready, left)

    def forward(data):
        first = jnp.dot(fwd[0], data, preferred_element_type=jnp.float32)
        return first + jnp.dot(fwd[1], data, preferred_element_type=jnp.float32)

    def inverse():
        high, low = r_high[...], r_low[...]
        first = jnp.dot(inv[0], high, preferred_element_type=jnp.float32)
        second = jnp.dot(inv[1], high, preferred_element_type=jnp.float32)
        return first + (second + jnp.dot(inv[0], low, preferred_element_type=jnp.float32))

    def over_chunks(body):
        steps = block // 2 // CHUNK
        for sign, start in ((1.0, 0), (-1.0, steps)):
            def step(index, carry, sign=sign):
                row = pl.multiple_of(index * CHUNK, CHUNK)
                re, im = pl.ds(row, CHUNK), pl.ds(row + block, CHUNK)
                real, imag = body(re, im, sign)
                for place, value in ((re, real), (im, imag)):
                    top = value.astype(jnp.bfloat16)
                    r_high[place, :] = top
                    r_low[place, :] = (value - top.astype(jnp.float32)).astype(jnp.bfloat16)
                return carry
            lax.fori_loop(start, start + steps, step, 0)

    def against(a, b):
        return a[0] * b[0] + a[1] * b[1], a[1] * b[0] - a[0] * b[1]

    def plus(a, b):
        return a[0] + b[0], a[1] + b[1]

    def pair_sum(grads, values, c, pairs, re, im):
        total = None
        for i, j in pairs:
            term = against(
                (grads[i, c, re, :], grads[i, c, im, :]), (values[j, c, re, :], values[j, c, im, :])
            )
            total = term if total is None else plus(total, term)
        return total

    def lags_spectrum(c, near, far):
        def body(re, im, sign):
            total = pair_sum(g_spec, u_spec, c, near, re, im)
            if far:
                real, imag = pair_sum(g_spec, u_spec, c, far, re, im)
                total = total[0] - sign * imag, total[1] + sign * real
            return total
        over_chunks(body)
        return inverse()

    def in_grad(c, terms):
        def body(re, im, sign):
            taps = [(tap_spec[s, c, re, :], tap_spec[s, c, im, :]) for s in range(segs)]
            total = None
            for d in range(terms):
                real = imag = 0.0
                if d < segs:
                    real, imag = taps[d]
                if d > 0:
                    real = real + sign * taps[d - 1][1]
                    imag = imag - sign * taps[d - 1][0]
                term = against((g_spec[d, c, re, :], g_spec[d, c, im, :]), (real, imag))
                total = term if total is None else plus(total, term)
            return total
        over_chunks(body)
        in_buf[c] = inverse().astype(jnp.bfloat16)
        pltpu.make_async_copy(in_buf.at[c, mine, :], out_ref.at[:, cols(side, c)], out_sem.at[0]).start()
        remote(in_buf.at[c, other, :], out_ref.at[:, cols(side, c)], send_sem.at[0], out_sem.at[0], mate)

    def send_lags(c, at, owner_level, slot):
        for who in range(pair):
            owner = owner_level * pair + who
            piece = part.at[c, pl.ds(owner * own_lags, own_lags), :]
            target = lag_ref.at[slot, :, cols(side, c)]
            if owner_level != at:
                remote(piece, target, send_sem.at[2], lag_sem.at[slot], owner)
        if owner_level == at:
            def piece_of(owner):
                return part.at[c, rows(owner, own_lags), :]
            target = lag_ref.at[slot, :, cols(side, c)]
            remote(piece_of(mate), target, send_sem.at[2], lag_sem.at[slot], mate)
            pltpu.make_async_copy(piece_of(me), target, lag_sem.at[slot]).start()

    def tap_chunk(c):
        for s in range(segs):
            data = tap_buf[s * block:(s + 1) * block, c * width:(c + 1) * width]
            tap_spec[s, c] = forward(data)

    pltpu.make_async_copy(fwd_hbm, fwd, local_sem.at[0]).wait()
    wait_for(tap_buf, local_sem.at[1])
    tap_chunk(0)

    @at_level(0)
    def _():
        pl.semaphore_wait(ready, 1)
        for c in range(chunks):
            remote(in_ref.at[:, cols(side, c)], u_buf.at[1, c, mine, :], send_sem.at[1], left_u_sem.at[c], right)

    for c in range(1, chunks):
        tap_chunk(c)
    pltpu.make_async_copy(inv_hbm, inv, local_sem.at[2]).wait()

    def own_grads(c, at):
        wait_for(g_buf.at[0, c], gx_sem.at[c])
        if at > 0:
            remote(g_buf.at[0, c, other, :], g_buf.at[1, c, other, :], send_sem.at[1], passed_sem.at[c], left)
        g_spec[0, c] = forward(g_buf[0, c])

    def own_values(c, at):
        wait_for(u_buf.at[0, c], ux_sem.at[c])
        if at == 0:
            remote(u_buf.at[0, c, other, :], u_buf.at[1, c, other, :], send_sem.at[1], left_u_sem.at[c], right)
        u_spec[0, c] = forward(u_buf[0, c])

    def direct_grads(c, at):
        wait_for(g_buf.at[1, c, mine, :], direct_sem.at[c])
        if at > 0:
            remote(g_buf.at[1, c, mine, :], g_buf.at[2, c, mine, :], send_sem.at[1], far_sem.at[c], left)

    def passed_grads(c, at):
        wait_for(g_buf.at[1, c, other, :], passed_sem.at[c])
        if at > 0:
            remote(g_buf.at[1, c, other, :], g_buf.at[2, c, other, :], send_sem.at[1], far_sem.at[c], left)
        g_spec[1, c] = forward(g_buf[1, c])

    def far_grads(c):
        wait_for(g_buf.at[2, c], far_sem.at[c])
        g_spec[2, c] = forward(g_buf[2, c])

    def left_values(c):
        wait_for(u_buf.at[1, c], left_u_sem.at[c])
        u_spec[1, c] = forward(u_buf[1, c])

    every = range(chunks)
    low_rows, high_rows = pl.ds(0, block), pl.ds(block, block)

    @at_level(0)
    def _():
        for c in every:
            own_grads(c, 0)
        for c in every:
            own_values(c, 0)
            direct_grads(c, 0)
            passed_grads(c, 0)
            part[c, low_rows, :] = lags_spectrum(c, [(0, 0)], []).astype(jnp.bfloat16)
            send_lags(c, 0, 1, 0)
            send_lags(c, 0, 0, 0)
        for c in every:
            far_grads(c)
            in_grad(c, 3)

    @at_level(1)
    def _():
        for c in every:
            own_grads(c, 1)
        for c in every:
            direct_grads(c, 1)
            own_values(c, 1)
            passed_grads(c, 1)
        for c in every:
            left_values(c)
        signal(ready_far, right)
        for c in every:
            part[c, low_rows, :] = lags_spectrum(c, [(0, 0)], [(1, 0), (0, 1)]).astype(jnp.bfloat16)
            send_lags(c, 1, 0, 1)
            send_lags(c, 1, 1, 1)
        for c in every:
            far_grads(c)
            part[c, high_rows, :] = lags_spectrum(
                c, [(1, 0), (0, 1)], [(2, 0), (1, 1)]
            ).astype(jnp.bfloat16)
            send_lags(c, 1, 3, 0)
            send_lags(c, 1, 2, 0)
            in_grad(c, 3)

    @at_level(2)
    def _():
        lag_ref[2] = jnp.zeros(lag_ref.shape[1:], lag_ref.dtype)
        for c in every:
            own_grads(c, 2)
        for c in every:
            direct_grads(c, 2)
            own_values(c, 2)
            passed_grads(c, 2)
        for c in every:
            own_low[c] = lags_spectrum(c, [(0, 0)], [(1, 0)])
        pl.semaphore_wait(ready_far, 1)

        def finish_low(c):
            wait_for(next_low.at[c], low_sem.at[c])
            part[c, low_rows, :] = (own_low[c] + next_low[c].astype(jnp.float32)).astype(jnp.bfloat16)
            send_lags(c, 2, 0, 2)
            send_lags(c, 2, 1, 2)

        finish_low(0)
        for c in every:
            part[c, high_rows, :] = lags_spectrum(c, [(1, 0)], []).astype(jnp.bfloat16)
            send_lags(c, 2, 3, 1)
            send_lags(c, 2, 2, 1)
        for c in every[1:]:
            in_grad(c - 1, 2)
            finish_low(c)
        in_grad(chunks - 1, 2)

    @at_level(3)
    def _():
        lag_ref[2] = jnp.zeros(lag_ref.shape[1:], lag_ref.dtype)
        for c in every:
            own_grads(c, 3)
        for c in every:
            own_values(c, 3)
            part[c, low_rows, :] = lags_spectrum(c, [(0, 0)], []).astype(jnp.bfloat16)
            remote(part.at[c, low_rows, :], next_low.at[c], send_sem.at[1], low_sem.at[c], left)
        for c in every:
            in_grad(c, 1)

    wait_for(out_ref, out_sem.at[0])
    wait_for(lag_ref.at[0], lag_sem.at[0])
    wait_for(lag_ref.at[1], lag_sem.at[1])

    @at_level(0, 1)
    def _():
        wait_for(lag_ref.at[2], lag_sem.at[2])

    wait_for(g_buf.at[:, :, pl.ds(0, tok_len), :], send_sem.at[0])

    @at_level(0)
    def _():
        wait_for(g_buf.at[0], send_sem.at[1])
        wait_for(part.at[:, pl.ds(0, (levels // 2 * pair - 1) * own_lags), :], send_sem.at[2])

    @at_level(1, 2, 3)
    def _():
        wait_for(g_buf.at[pl.ds(0, 2)], send_sem.at[1])

    @at_level(1, 2)
    def _():
        wait_for(part.at[:, pl.ds(0, (levels * pair - 1) * own_lags), :], send_sem.at[2])


def rows_of_half(side, half):
    return pl.ds(pl.multiple_of(side * half, LANES), half)


def finish_kernel(in_ref, lag_ref, in_out, lag_out, lag_wide, sem):
    move = pltpu.make_async_copy(in_ref, in_out, sem.at[0])
    move.start()
    wide = [lag_ref[slot].astype(lag_wide.dtype) for slot in range(lag_ref.shape[0])]
    lag_wide[...] = wide[0] + wide[1] + wide[2]
    store = pltpu.make_async_copy(lag_wide, lag_out, sem.at[1])
    store.start()
    move.wait()
    store.wait()


PAIR = 2


def chain_fits(tok_len, channels, lag_count, count):
    block = PAIR * tok_len
    return (
        count % PAIR == 0
        and lag_count == 2 * block
        and count // PAIR == 2 * (lag_count // block)
        and channels % (PAIR * CHUNKS * LANES) == 0
        and tok_len % (2 * CHUNK) == 0
        and lag_count % (count * CHUNK) == 0
    )


def per_device(inputs, out_grad, filters):
    tok_len, channels = out_grad.shape
    lag_count = filters.shape[0]
    count = lax.axis_size("ctx")
    if not chain_fits(tok_len, channels, lag_count, count):
        return general_plan(inputs, out_grad, filters)
    block = PAIR * tok_len
    segs = lag_count // block
    half = channels // PAIR
    width = half // CHUNKS
    own_lags = lag_count // count
    fwd, inv = transform_tables(block)
    bf16, f32 = jnp.bfloat16, jnp.float32
    dma = pltpu.SemaphoreType.DMA
    anywhere = pl.BlockSpec(memory_space=pl.ANY)
    in_vmem = pl.BlockSpec(memory_space=pltpu.VMEM)
    in_grad, lag_grad = pl.pallas_call(
        functools.partial(chain_kernel, PAIR, block, CHUNKS),
        out_shape=(
            pltpu.VMEM((tok_len, channels), bf16),
            pltpu.VMEM((3, own_lags, channels), bf16),
        ),
        in_specs=[anywhere] * 5,
        out_specs=(in_vmem, in_vmem),
        scratch_shapes=[
            pltpu.VMEM((3, CHUNKS, block, width), bf16),
            pltpu.VMEM((2, CHUNKS, block, width), bf16),
            pltpu.VMEM((lag_count, half), bf16),
            pltpu.VMEM(fwd.shape, bf16),
            pltpu.VMEM(inv.shape, bf16),
            pltpu.VMEM((3, CHUNKS, 2 * block, width), f32),
            pltpu.VMEM((2, CHUNKS, 2 * block, width), f32),
            pltpu.VMEM((segs, CHUNKS, 2 * block, width), f32),
            pltpu.VMEM((2 * block, width), bf16),
            pltpu.VMEM((2 * block, width), bf16),
            pltpu.VMEM((CHUNKS, block, width), bf16),
            pltpu.VMEM((CHUNKS, lag_count, width), bf16),
            pltpu.VMEM((CHUNKS, block, width), f32),
            pltpu.VMEM((CHUNKS, block, width), bf16),
            dma((CHUNKS,)), dma((CHUNKS,)), dma((CHUNKS,)), dma((CHUNKS,)), dma((CHUNKS,)),
            dma((CHUNKS,)), dma((CHUNKS,)), dma((3,)), dma((1,)), dma((3,)), dma((3,)),
            pltpu.SemaphoreType.REGULAR,
            pltpu.SemaphoreType.REGULAR,
        ],
        compiler_params=pltpu.CompilerParams(collective_id=0, has_side_effects=True),
    )(inputs, out_grad, filters, jnp.asarray(fwd), jnp.asarray(inv))
    return pl.pallas_call(
        finish_kernel,
        out_shape=(
            jax.ShapeDtypeStruct(in_grad.shape, bf16),
            jax.ShapeDtypeStruct(lag_grad.shape[1:], f32),
        ),
        in_specs=[in_vmem, in_vmem],
        out_specs=(anywhere, anywhere),
        scratch_shapes=[
            pltpu.VMEM(lag_grad.shape[1:], f32),
            pltpu.SemaphoreType.DMA((2,)),
        ],
    )(
        pltpu.with_memory_space_constraint(in_grad, pltpu.VMEM),
        pltpu.with_memory_space_constraint(lag_grad, pltpu.VMEM),
    )


def solution(mesh):
    return jax.shard_map(
        per_device,
        mesh=mesh,
        in_specs=(P(("groups", "ctx"), "chan"), P(("groups", "ctx"), "chan"), P(None, "chan")),
        out_specs=(P(("groups", "ctx"), "chan"), P(("groups", "ctx"), "chan")),
        check_vma=False,
    )
```

```python
import functools
import math

import jax
import jax.numpy as jnp
import numpy as np
from jax import lax
from jax.experimental import pallas as pl
from jax.experimental.pallas import tpu as pltpu
from jax.sharding import PartitionSpec as P

LANES = 128
CHUNK = 16
CHUNKS = 2
FORWARD_PASSES = 1
TAP_PASSES = 2
INVERSE_PASSES = 1


def passed_along(value, axis, steps):
    count = lax.axis_size(axis)
    initial, last = (max(0, -steps), min(count, count - steps))
    return lax.ppermute(value, axis, [(source, source + steps) for source in range(initial, last)])


def phase_table(row_ids, col_ids, period):
    return 2.0 * math.pi / period * (row_ids * col_ids % period).astype(jnp.float32)


def split_table(table):
    high_part = table.astype(jnp.bfloat16)
    low_part = (table - high_part.astype(jnp.float32)).astype(jnp.bfloat16)
    return (high_part, low_part)


def forward_apply(parts, data):
    first = jnp.dot(parts[0], data, preferred_element_type=jnp.float32)
    return first + jnp.dot(parts[1], data, preferred_element_type=jnp.float32)


def spectral(table, data):
    return jnp.dot(table, data, precision=lax.Precision.HIGH, preferred_element_type=jnp.float32)


def general_plan(inputs, out_grad, filters):
    tok_len = out_grad.shape[0]
    channels = out_grad.shape[1]
    lag_count = filters.shape[0]
    far_reach = lag_count // tok_len
    period = 2 * tok_len
    freq_count = tok_len + 1
    freq_col = jnp.arange(freq_count, dtype=jnp.int32)[:, None]
    time_row = jnp.arange(tok_len, dtype=jnp.int32)[None, :]
    angle_fwd = phase_table(freq_col, time_row, period)
    forward = split_table(jnp.concatenate([jnp.cos(angle_fwd), -jnp.sin(angle_fwd)], axis=0))
    freq_row = jnp.arange(freq_count, dtype=jnp.int32)[None, :]
    weighting = (
        jnp.where((freq_row == 0) | (freq_row == tok_len), 1.0, 2.0).astype(jnp.float32) / period
    )
    back_rows = (tok_len - jnp.arange(tok_len, dtype=jnp.int32))[:, None]
    angle_back = phase_table(back_rows, freq_row, period)
    inverse_in = jnp.concatenate(
        [weighting * jnp.cos(angle_back), -weighting * jnp.sin(angle_back)], axis=1
    )
    lag_rows = ((jnp.arange(period, dtype=jnp.int32) - tok_len) % period)[:, None]
    angle_lag = phase_table(lag_rows, freq_row, period)
    inverse_lag = jnp.concatenate(
        [weighting * jnp.cos(angle_lag), -weighting * jnp.sin(angle_lag)], axis=1
    )
    parity = jnp.where(jnp.arange(freq_count) % 2 == 0, 1.0, -1.0).astype(jnp.float32)
    parity_both = jnp.concatenate([parity, parity])[:, None]
    received = [out_grad]
    current = out_grad
    for offset in range(far_reach):
        current = passed_along(current, "ctx", -1)
        received.append(current)
    tap_blocks = filters.reshape(far_reach, tok_len, channels)
    tap_spec = jnp.einsum("ft,btc->bfc", forward[0], tap_blocks, preferred_element_type=jnp.float32)
    tap_spec = tap_spec + jnp.einsum(
        "ft,btc->bfc", forward[1], tap_blocks, preferred_element_type=jnp.float32
    )
    input_spec = forward_apply(forward, inputs)
    input_re = input_spec[:freq_count]
    input_im = input_spec[freq_count:]
    accum_re = jnp.zeros((freq_count, channels), jnp.float32)
    accum_im = jnp.zeros((freq_count, channels), jnp.float32)
    lag_parts = []
    for offset in range(far_reach + 1):
        grad_spec = forward_apply(forward, received[offset])
        grad_re = grad_spec[:freq_count]
        grad_im = grad_spec[freq_count:]
        if offset >= 1 and offset < far_reach:
            segment = tap_spec[offset - 1] + parity_both * tap_spec[offset]
        elif offset >= 1:
            segment = tap_spec[offset - 1]
        else:
            segment = parity_both * tap_spec[offset]
        seg_re = segment[:freq_count]
        seg_im = segment[freq_count:]
        accum_re = accum_re + grad_re * seg_re + grad_im * seg_im
        accum_im = accum_im + grad_re * seg_im - grad_im * seg_re
        cross = jnp.concatenate(
            [grad_re * input_re + grad_im * input_im, grad_im * input_re - grad_re * input_im],
            axis=0,
        )
        lag_parts.append(spectral(inverse_lag, cross))
    in_grad = spectral(inverse_in, jnp.concatenate([accum_re, accum_im], axis=0)).astype(
        jnp.bfloat16
    )
    segments = [
        lag_parts[index + 1][:tok_len] + lag_parts[index][tok_len:] for index in range(far_reach)
    ]
    partial_value = jnp.concatenate(segments, axis=0)
    filter_grad = lax.psum_scatter(partial_value, "ctx", scatter_dimension=0, tiled=True)
    return (in_grad, filter_grad)


def table_parts(table):
    high_part = table.astype(jnp.bfloat16)
    low_part = (table - high_part.astype(np.float64)).astype(jnp.bfloat16)
    return np.stack([high_part, low_part])


def transform_tables(block):
    order = np.concatenate([np.arange(0, block, 2), np.arange(1, block, 2)])
    steps = (2 * order + 1)[:, None] * np.arange(block)[None, :] % (4 * block)
    angle = np.pi / (2 * block) * steps
    forward = np.concatenate([np.cos(angle), np.sin(angle)], axis=0)
    return table_parts(forward), table_parts(forward.T / block)


def wait_for(like, sem):
    pltpu.make_async_copy(like, like, sem).wait()


def chain_kernel(
    pair, block, chunks,
    in_ref, grad_ref, taps_ref, fwd_hbm, inv_hbm,
    out_ref, lag_ref,
    g_buf, u_buf, g_send, u_send, tap_buf, fwd, inv, g_spec, u_spec, tap_spec, r_high, r_low, in_buf, far_buf, in_sum, part, own_low, next_low,
    gx_sem, ux_sem, direct_sem, passed_sem, far_sem, left_u_sem, low_sem, lag_sem, out_sem, send_sem, local_sem,
    right_in, pair_in, far_in,
):
    me = lax.axis_index("ctx")
    level = lax.div(me, pair)
    side = lax.rem(me, pair)
    mate = me + 1 - 2 * side
    left, right = me - pair, me + pair
    tok_len, channels = in_ref.shape
    lag_count = taps_ref.shape[0]
    width = g_buf.shape[3]
    half = chunks * width
    segs = lag_count // block
    levels = 2 * segs
    own_lags = lag_count // (levels * pair)

    def cols(which, c):
        return pl.ds(pl.multiple_of(which * half + c * width, LANES), width)

    def rows(which, length):
        return pl.ds(pl.multiple_of(which * length, length), length)

    mine, other = rows(side, tok_len), rows(1 - side, tok_len)

    def remote(source, target, send, recv, device):
        pltpu.make_async_remote_copy(
            src_ref=source, dst_ref=target, send_sem=send, recv_sem=recv,
            device_id={"ctx": device}, device_id_type=pl.DeviceIdType.MESH,
        ).start()

    def signal(sem, device):
        pl.semaphore_signal(
            sem, inc=1, device_id={"ctx": device}, device_id_type=pl.DeviceIdType.MESH
        )

    def at_level(*which):
        hit = level == which[0]
        for value in which[1:]:
            hit = jnp.logical_or(hit, level == value)
        return pl.when(hit)

    barrier = pltpu.get_barrier_semaphore()
    signal(barrier, mate)

    @pl.when(level < levels - 1)
    def _():
        signal(barrier, right)

    every = range(chunks)
    whole = chunks // 2
    for source, kept, sent, sem in (
        (grad_ref, g_buf, g_send, local_sem.at[3]), (in_ref, u_buf, u_send, local_sem.at[4])
    ):
        for c in every:
            pltpu.make_async_copy(source.at[:, cols(1 - side, c)], sent.at[c], sem).start()
            pltpu.make_async_copy(source.at[:, cols(side, c)], kept.at[0, c, mine, :], sem).start()
    pltpu.make_async_copy(fwd_hbm, fwd, local_sem.at[0]).start()
    pltpu.make_async_copy(taps_ref.at[:, rows_of_half(side, half)], tap_buf, local_sem.at[1]).start()
    pltpu.make_async_copy(inv_hbm, inv, local_sem.at[2]).start()

    pl.semaphore_wait(barrier, 1 + jnp.minimum(level, 1))

    def mate_grads(c):
        remote(g_send.at[c], g_buf.at[0, c, mine, :], send_sem.at[0], gx_sem.at[c], mate)

    def mate_values(c):
        remote(u_send.at[c], u_buf.at[0, c, mine, :], send_sem.at[0], ux_sem.at[c], mate)

    def grads_left(c):
        remote(g_buf.at[0, c, mine, :], g_buf.at[1, c, mine, :], send_sem.at[1], direct_sem.at[c], left)

    def values_right(c):
        remote(u_buf.at[0, c, mine, :], u_buf.at[1, c, mine, :], send_sem.at[1], left_u_sem.at[c], right)

    wait_for(g_buf.at[0], local_sem.at[3])

    def forward(data, passes=FORWARD_PASSES):
        total = jnp.dot(fwd[0], data, preferred_element_type=jnp.float32)
        if passes > 1:
            total = total + jnp.dot(fwd[1], data, preferred_element_type=jnp.float32)
        return total

    def inverse():
        total = jnp.dot(inv[0], r_high[...], preferred_element_type=jnp.float32)
        if INVERSE_PASSES > 1:
            total = total + jnp.dot(inv[1], r_high[...], preferred_element_type=jnp.float32)
        if INVERSE_PASSES > 2:
            total = total + jnp.dot(inv[0], r_low[...], preferred_element_type=jnp.float32)
        return total

    def over_chunks(body):
        steps = block // 2 // CHUNK
        for sign, start in ((1.0, 0), (-1.0, steps)):
            def step(index, carry, sign=sign):
                row = pl.multiple_of(index * CHUNK, CHUNK)
                re, im = pl.ds(row, CHUNK), pl.ds(row + block, CHUNK)
                real, imag = body(re, im, sign)
                for place, value in ((re, real), (im, imag)):
                    top = value.astype(jnp.bfloat16)
                    r_high[place, :] = top
                    if INVERSE_PASSES > 2:
                        r_low[place, :] = (value - top.astype(jnp.float32)).astype(jnp.bfloat16)
                return carry
            lax.fori_loop(start, start + steps, step, 0)

    def against(a, b):
        return a[0] * b[0] + a[1] * b[1], a[1] * b[0] - a[0] * b[1]

    def plus(a, b):
        return a[0] + b[0], a[1] + b[1]

    def pair_sum(grads, values, c, pairs, re, im):
        total = None
        for i, j in pairs:
            term = against(
                (grads[i, c, re, :], grads[i, c, im, :]), (values[j, c, re, :], values[j, c, im, :])
            )
            total = term if total is None else plus(total, term)
        return total

    def lags_spectrum(c, near, far):
        def body(re, im, sign):
            total = pair_sum(g_spec, u_spec, c, near, re, im)
            if far:
                real, imag = pair_sum(g_spec, u_spec, c, far, re, im)
                total = total[0] - sign * imag, total[1] + sign * real
            return total
        over_chunks(body)
        return inverse()

    def in_terms(c, terms):
        def body(re, im, sign):
            taps = [(tap_spec[s, c, re, :], tap_spec[s, c, im, :]) for s in range(segs)]
            total = None
            for i, d in terms:
                real = imag = 0.0
                if d < segs:
                    real, imag = taps[d]
                if d > 0:
                    real = real + sign * taps[d - 1][1]
                    imag = imag - sign * taps[d - 1][0]
                term = against((g_spec[i, c, re, :], g_spec[i, c, im, :]), (real, imag))
                total = term if total is None else plus(total, term)
            return total
        over_chunks(body)
        return inverse().astype(jnp.bfloat16)

    def out_place(c):
        return out_ref.at[:, cols(side, c)]

    def in_grad(c, terms, target):
        in_buf[c] = in_terms(c, terms)
        place = target
        remote(in_buf.at[c, other, :], place, send_sem.at[0], out_sem.at[0], mate)
        pltpu.make_async_copy(in_buf.at[c, mine, :], place, out_sem.at[0]).start()

    def send_lags(c, at, owner_level, slot):
        for who in range(pair):
            owner = owner_level * pair + who
            piece = part.at[c, pl.ds(owner * own_lags, own_lags), :]
            target = lag_ref.at[slot, :, cols(side, c)]
            if owner_level != at:
                remote(piece, target, send_sem.at[2], lag_sem.at[slot], owner)
        if owner_level == at:
            def piece_of(owner):
                return part.at[c, rows(owner, own_lags), :]
            target = lag_ref.at[slot, :, cols(side, c)]
            remote(piece_of(mate), target, send_sem.at[2], lag_sem.at[slot], mate)
            pltpu.make_async_copy(piece_of(me), target, lag_sem.at[slot]).start()

    def tap_chunk(c):
        for s in range(segs):
            data = tap_buf[s * block:(s + 1) * block, c * width:(c + 1) * width]
            tap_spec[s, c] = forward(data, TAP_PASSES)

    @at_level(1, 2)
    def _():
        signal(right_in, left)

    @at_level(1, 2, 3)
    def _():
        for c in every:
            mate_grads(c)

            if c < whole:
                grads_left(c)
            else:
                @at_level(2, 3)
                def _():
                    grads_left(c)

    wait_for(u_buf.at[0], local_sem.at[4])
    for c in every:
        mate_values(c)

    @at_level(0)
    def _():
        for c in every:
            mate_grads(c)

    pltpu.make_async_copy(fwd_hbm, fwd, local_sem.at[0]).wait()
    wait_for(tap_buf, local_sem.at[1])
    tap_chunk(0)

    @at_level(0, 1)
    def _():
        pl.semaphore_wait(right_in, 1)
        for c in every:
            values_right(c)

        @at_level(0)
        def _():
            signal(pair_in, right)

    for c in every[1:]:
        tap_chunk(c)

    @at_level(1)
    def _():
        pl.semaphore_wait(pair_in, 1)
        signal(far_in, right)

    pltpu.make_async_copy(inv_hbm, inv, local_sem.at[2]).wait()

    def own_grads(c, pass_on):
        wait_for(g_buf.at[0, c, other, :], gx_sem.at[c])
        if pass_on:
            remote(g_buf.at[0, c, other, :], g_buf.at[1, c, other, :], send_sem.at[1], passed_sem.at[c], left)

    def own_values(c, pass_on):
        wait_for(u_buf.at[0, c, other, :], ux_sem.at[c])
        if pass_on:
            remote(u_buf.at[0, c, other, :], u_buf.at[1, c, other, :], send_sem.at[1], left_u_sem.at[c], right)

    def direct_grads(c, pass_on):
        wait_for(g_buf.at[1, c, mine, :], direct_sem.at[c])
        if pass_on:
            remote(g_buf.at[1, c, mine, :], g_buf.at[2, c, mine, :], send_sem.at[1], far_sem.at[c], left)

    def passed_grads(c, pass_on):
        wait_for(g_buf.at[1, c, other, :], passed_sem.at[c])
        if pass_on:
            remote(g_buf.at[1, c, other, :], g_buf.at[2, c, other, :], send_sem.at[1], far_sem.at[c], left)

    def grads_spectrum(i, c):
        g_spec[i, c] = forward(g_buf[i, c])

    def values_spectrum(i, c):
        u_spec[i, c] = forward(u_buf[i, c])

    def far_grads(c):
        wait_for(g_buf.at[2, c], far_sem.at[c])
        grads_spectrum(2, c)

    def left_values(c):
        wait_for(u_buf.at[1, c], left_u_sem.at[c])
        values_spectrum(1, c)

    low_rows, high_rows = pl.ds(0, block), pl.ds(block, block)
    low_owners = levels // 2 * pair
    turns = [
        (c, owner) for first in range(0, low_owners, pair) for c in every for owner in range(first, first + pair)
    ]

    @at_level(0)
    def _():
        for c in every:
            own_values(c, True)
            values_spectrum(0, c)
        for c in every:
            own_grads(c, False)
            grads_spectrum(0, c)
            part[c, low_rows, :] = lags_spectrum(c, [(0, 0)], []).astype(jnp.bfloat16)
            send_lags(c, 0, 0, 0)
        for c in every[whole:]:
            in_grad(c, [(0, 0)], in_sum.at[0, side, c - whole])
        for c in every[:whole]:
            direct_grads(c, False)
            passed_grads(c, False)
            grads_spectrum(1, c)
        for c in every:
            send_lags(c, 0, 1, 0)
        for c in every[:whole]:
            far_grads(c)
            in_grad(c, [(0, 0), (1, 1), (2, 2)], out_place(c))

    @at_level(1)
    def _():
        for c in every:
            own_grads(c, c < whole)
            grads_spectrum(0, c)
        for c in every:
            direct_grads(c, c < whole)
        for c in every:
            own_values(c, True)
            values_spectrum(0, c)

        def low(c):
            left_values(c)
            part[c, low_rows, :] = lags_spectrum(c, [(0, 0)], [(0, 1)]).astype(jnp.bfloat16)
            low_to(c, 0)

        def low_to(c, owner):
            piece = part.at[c, pl.ds(owner * own_lags, own_lags), :]
            remote(piece, lag_ref.at[1, :, cols(side, c)], send_sem.at[2], lag_sem.at[1], owner)

        def far_to(c, owner):
            remote(
                far_buf.at[c - whole, pl.ds(owner * tok_len, tok_len), :], in_sum.at[1, side, c - whole],
                send_sem.at[3], out_sem.at[1], owner,
            )

        def passed(c):
            passed_grads(c, c < whole)
            grads_spectrum(1, c)
            if c >= whole:
                far_buf[c - whole] = in_terms(c, [(0, 1), (1, 2)])
                far_to(c, 0)

        low(0)
        for c in every[1:]:
            passed(c - 1)
            low(c)
        passed(chunks - 1)
        for owner in range(1, pair):
            for c in every[whole:]:
                far_to(c, owner)
            for c in every:
                low_to(c, owner)
        for c in every:
            send_lags(c, 1, 1, 1)
        for c in every:
            part[c, high_rows, :] = lags_spectrum(c, [(0, 1)], [(1, 1)]).astype(jnp.bfloat16)
        for c in every:
            far_grads(c)
            send_lags(c, 1, 3, 0)
            send_lags(c, 1, 2, 0)
            in_grad(c, [(0, 0), (1, 1), (2, 2)], out_place(c))

    @at_level(2)
    def _():
        lag_ref[2] = jnp.zeros(lag_ref.shape[1:], lag_ref.dtype)
        for c in every:
            own_grads(c, True)
            grads_spectrum(0, c)
        direct_grads(0, True)
        for c in every:
            own_values(c, False)
            values_spectrum(0, c)
        for c in every:
            passed_grads(c, True)
            if c + 1 < chunks:
                direct_grads(c + 1, True)
            grads_spectrum(1, c)
            if c == 0:
                in_grad(0, [(0, 0), (1, 1)], out_place(0))
        for c in every:
            left_values(c)
            own_low[c] = lags_spectrum(c, [(0, 0)], [(1, 0), (0, 1)])
        pl.semaphore_wait(far_in, 1)

        def finish_low(c, owner):
            piece = pl.ds(owner * own_lags, own_lags)
            wait_for(next_low.at[c, piece, :], low_sem.at[c, owner])
            total = own_low[c, piece, :] + next_low[c, piece, :].astype(jnp.float32)
            part[c, piece, :] = total.astype(jnp.bfloat16)
            remote(part.at[c, piece, :], lag_ref.at[2, :, cols(side, c)], send_sem.at[2], lag_sem.at[2], owner)

        def high(c):
            part[c, high_rows, :] = lags_spectrum(c, [(1, 0), (0, 1)], [(1, 1)]).astype(jnp.bfloat16)
            send_lags(c, 2, 3, 1)
            send_lags(c, 2, 2, 1)

        half_way = len(turns) // 2
        for turn in sorted(turns[:half_way], key=lambda turn: turn[1]):
            finish_low(*turn)
        high(0)
        for turn in turns[half_way:]:
            finish_low(*turn)
        for c in every[1:]:
            high(c)
        for c in every[1:]:
            in_grad(c, [(0, 0), (1, 1)], out_place(c))

    @at_level(3)
    def _():
        lag_ref[2] = jnp.zeros(lag_ref.shape[1:], lag_ref.dtype)

        def next_level_low(c, owner):
            piece = pl.ds(owner * own_lags, own_lags)
            remote(part.at[c, piece, :], next_low.at[c, piece, :], send_sem.at[1], low_sem.at[c, owner], left)

        for c in every:
            own_grads(c, True)
            grads_spectrum(0, c)
        for c in every:
            own_values(c, False)
            values_spectrum(0, c)
            part[c, low_rows, :] = lags_spectrum(c, [(0, 0)], []).astype(jnp.bfloat16)
            for owner in range(pair):
                next_level_low(c, owner)
        for c, owner in turns[pair * chunks:]:
            next_level_low(c, owner)
        for c in every:
            in_grad(c, [(0, 0)], out_place(c))

    wait_for(out_ref, out_sem.at[0])

    @at_level(0)
    def _():
        wait_for(in_sum.at[1], out_sem.at[1])
        for which in range(pair):
            for c in every[whole:]:
                at = which * half + c * width
                total = in_sum[0, which, c - whole].astype(jnp.float32) + in_sum[1, which, c - whole].astype(jnp.float32)
                out_ref[:, at:at + width] = total.astype(out_ref.dtype)

    wait_for(lag_ref.at[0], lag_sem.at[0])
    wait_for(lag_ref.at[1], lag_sem.at[1])

    @at_level(0, 1)
    def _():
        wait_for(lag_ref.at[2], lag_sem.at[2])

    wait_for(g_buf.at[:, :, pl.ds(0, tok_len), :], send_sem.at[0])

    @at_level(0)
    def _():
        wait_for(g_buf.at[0], send_sem.at[1])
        wait_for(part.at[:, pl.ds(0, (levels // 2 * pair - 1) * own_lags), :], send_sem.at[2])

    @at_level(1, 2, 3)
    def _():
        wait_for(g_buf.at[pl.ds(0, 2)], send_sem.at[1])

    @at_level(1)
    def _():
        wait_for(far_buf, send_sem.at[3])

    @at_level(1, 2)
    def _():
        wait_for(part.at[:, pl.ds(0, (levels * pair - 1) * own_lags), :], send_sem.at[2])


def rows_of_half(side, half):
    return pl.ds(pl.multiple_of(side * half, LANES), half)


def finish_kernel(in_ref, lag_ref, in_out, lag_out, lag_wide, sem):
    move = pltpu.make_async_copy(in_ref, in_out, sem.at[0])
    move.start()
    wide = [lag_ref[slot].astype(lag_wide.dtype) for slot in range(lag_ref.shape[0])]
    lag_wide[...] = wide[0] + wide[1] + wide[2]
    store = pltpu.make_async_copy(lag_wide, lag_out, sem.at[1])
    store.start()
    move.wait()
    store.wait()


PAIR = 2


def chain_fits(tok_len, channels, lag_count, count):
    block = PAIR * tok_len
    return (
        count % PAIR == 0
        and lag_count == 2 * block
        and count // PAIR == 2 * (lag_count // block)
        and channels % (PAIR * CHUNKS * LANES) == 0
        and tok_len % (2 * CHUNK) == 0
        and lag_count % (count * CHUNK) == 0
    )


def per_device(inputs, out_grad, filters):
    tok_len, channels = out_grad.shape
    lag_count = filters.shape[0]
    count = lax.axis_size("ctx")
    if not chain_fits(tok_len, channels, lag_count, count):
        return general_plan(inputs, out_grad, filters)
    block = PAIR * tok_len
    segs = lag_count // block
    half = channels // PAIR
    width = half // CHUNKS
    own_lags = lag_count // count
    fwd, inv = transform_tables(block)
    bf16, f32 = jnp.bfloat16, jnp.float32
    dma = pltpu.SemaphoreType.DMA
    anywhere = pl.BlockSpec(memory_space=pl.ANY)
    in_vmem = pl.BlockSpec(memory_space=pltpu.VMEM)
    in_grad, lag_grad = pl.pallas_call(
        functools.partial(chain_kernel, PAIR, block, CHUNKS),
        out_shape=(
            pltpu.VMEM((tok_len, channels), bf16),
            pltpu.VMEM((3, own_lags, channels), bf16),
        ),
        in_specs=[anywhere] * 5,
        out_specs=(in_vmem, in_vmem),
        scratch_shapes=[
            pltpu.VMEM((3, CHUNKS, block, width), bf16),
            pltpu.VMEM((2, CHUNKS, block, width), bf16),
            pltpu.VMEM((CHUNKS, tok_len, width), bf16),
            pltpu.VMEM((CHUNKS, tok_len, width), bf16),
            pltpu.VMEM((lag_count, half), bf16),
            pltpu.VMEM(fwd.shape, bf16),
            pltpu.VMEM(inv.shape, bf16),
            pltpu.VMEM((3, CHUNKS, 2 * block, width), f32),
            pltpu.VMEM((2, CHUNKS, 2 * block, width), f32),
            pltpu.VMEM((segs, CHUNKS, 2 * block, width), f32),
            pltpu.VMEM((2 * block, width), bf16),
            pltpu.VMEM((2 * block, width), bf16),
            pltpu.VMEM((CHUNKS, block, width), bf16),
            pltpu.VMEM((CHUNKS // 2, block, width), bf16),
            pltpu.VMEM((2, PAIR, CHUNKS // 2, tok_len, width), bf16),
            pltpu.VMEM((CHUNKS, lag_count, width), bf16),
            pltpu.VMEM((CHUNKS, block, width), f32),
            pltpu.VMEM((CHUNKS, block, width), bf16),
            dma((CHUNKS,)), dma((CHUNKS,)), dma((CHUNKS,)), dma((CHUNKS,)), dma((CHUNKS,)),
            dma((CHUNKS,)), dma((CHUNKS, count // 2)), dma((3,)), dma((2,)), dma((4,)), dma((5,)),
            pltpu.SemaphoreType.REGULAR,
            pltpu.SemaphoreType.REGULAR,
            pltpu.SemaphoreType.REGULAR,
        ],
        compiler_params=pltpu.CompilerParams(collective_id=0, has_side_effects=True),
    )(inputs, out_grad, filters, jnp.asarray(fwd), jnp.asarray(inv))
    return pl.pallas_call(
        finish_kernel,
        out_shape=(
            jax.ShapeDtypeStruct(in_grad.shape, bf16),
            jax.ShapeDtypeStruct(lag_grad.shape[1:], f32),
        ),
        in_specs=[in_vmem, in_vmem],
        out_specs=(anywhere, anywhere),
        scratch_shapes=[
            pltpu.VMEM(lag_grad.shape[1:], f32),
            pltpu.SemaphoreType.DMA((2,)),
        ],
    )(
        pltpu.with_memory_space_constraint(in_grad, pltpu.VMEM),
        pltpu.with_memory_space_constraint(lag_grad, pltpu.VMEM),
    )


def solution(mesh):
    return jax.shard_map(
        per_device,
        mesh=mesh,
        in_specs=(P(("groups", "ctx"), "chan"), P(("groups", "ctx"), "chan"), P(None, "chan")),
        out_specs=(P(("groups", "ctx"), "chan"), P(("groups", "ctx"), "chan")),
        check_vma=False,
    )
```

```python
import functools
import math

import jax
import jax.numpy as jnp
import numpy as np
from jax import lax
from jax.experimental import pallas as pl
from jax.experimental.pallas import tpu as pltpu
from jax.sharding import PartitionSpec as P

LANES = 128
CHUNK = 16
CHUNKS = 2
FORWARD_PASSES = 1
TAP_PASSES = 2
INVERSE_PASSES = 1


def passed_along(value, axis, steps):
    count = lax.axis_size(axis)
    initial, last = (max(0, -steps), min(count, count - steps))
    return lax.ppermute(value, axis, [(source, source + steps) for source in range(initial, last)])


def phase_table(row_ids, col_ids, period):
    return 2.0 * math.pi / period * (row_ids * col_ids % period).astype(jnp.float32)


def split_table(table):
    high_part = table.astype(jnp.bfloat16)
    low_part = (table - high_part.astype(jnp.float32)).astype(jnp.bfloat16)
    return (high_part, low_part)


def forward_apply(parts, data):
    first = jnp.dot(parts[0], data, preferred_element_type=jnp.float32)
    return first + jnp.dot(parts[1], data, preferred_element_type=jnp.float32)


def spectral(table, data):
    return jnp.dot(table, data, precision=lax.Precision.HIGH, preferred_element_type=jnp.float32)


def general_plan(inputs, out_grad, filters):
    tok_len = out_grad.shape[0]
    channels = out_grad.shape[1]
    lag_count = filters.shape[0]
    far_reach = lag_count // tok_len
    period = 2 * tok_len
    freq_count = tok_len + 1
    freq_col = jnp.arange(freq_count, dtype=jnp.int32)[:, None]
    time_row = jnp.arange(tok_len, dtype=jnp.int32)[None, :]
    angle_fwd = phase_table(freq_col, time_row, period)
    forward = split_table(jnp.concatenate([jnp.cos(angle_fwd), -jnp.sin(angle_fwd)], axis=0))
    freq_row = jnp.arange(freq_count, dtype=jnp.int32)[None, :]
    weighting = (
        jnp.where((freq_row == 0) | (freq_row == tok_len), 1.0, 2.0).astype(jnp.float32) / period
    )
    back_rows = (tok_len - jnp.arange(tok_len, dtype=jnp.int32))[:, None]
    angle_back = phase_table(back_rows, freq_row, period)
    inverse_in = jnp.concatenate(
        [weighting * jnp.cos(angle_back), -weighting * jnp.sin(angle_back)], axis=1
    )
    lag_rows = ((jnp.arange(period, dtype=jnp.int32) - tok_len) % period)[:, None]
    angle_lag = phase_table(lag_rows, freq_row, period)
    inverse_lag = jnp.concatenate(
        [weighting * jnp.cos(angle_lag), -weighting * jnp.sin(angle_lag)], axis=1
    )
    parity = jnp.where(jnp.arange(freq_count) % 2 == 0, 1.0, -1.0).astype(jnp.float32)
    parity_both = jnp.concatenate([parity, parity])[:, None]
    received = [out_grad]
    current = out_grad
    for offset in range(far_reach):
        current = passed_along(current, "ctx", -1)
        received.append(current)
    tap_blocks = filters.reshape(far_reach, tok_len, channels)
    tap_spec = jnp.einsum("ft,btc->bfc", forward[0], tap_blocks, preferred_element_type=jnp.float32)
    tap_spec = tap_spec + jnp.einsum(
        "ft,btc->bfc", forward[1], tap_blocks, preferred_element_type=jnp.float32
    )
    input_spec = forward_apply(forward, inputs)
    input_re = input_spec[:freq_count]
    input_im = input_spec[freq_count:]
    accum_re = jnp.zeros((freq_count, channels), jnp.float32)
    accum_im = jnp.zeros((freq_count, channels), jnp.float32)
    lag_parts = []
    for offset in range(far_reach + 1):
        grad_spec = forward_apply(forward, received[offset])
        grad_re = grad_spec[:freq_count]
        grad_im = grad_spec[freq_count:]
        if offset >= 1 and offset < far_reach:
            segment = tap_spec[offset - 1] + parity_both * tap_spec[offset]
        elif offset >= 1:
            segment = tap_spec[offset - 1]
        else:
            segment = parity_both * tap_spec[offset]
        seg_re = segment[:freq_count]
        seg_im = segment[freq_count:]
        accum_re = accum_re + grad_re * seg_re + grad_im * seg_im
        accum_im = accum_im + grad_re * seg_im - grad_im * seg_re
        cross = jnp.concatenate(
            [grad_re * input_re + grad_im * input_im, grad_im * input_re - grad_re * input_im],
            axis=0,
        )
        lag_parts.append(spectral(inverse_lag, cross))
    in_grad = spectral(inverse_in, jnp.concatenate([accum_re, accum_im], axis=0)).astype(
        jnp.bfloat16
    )
    segments = [
        lag_parts[index + 1][:tok_len] + lag_parts[index][tok_len:] for index in range(far_reach)
    ]
    partial_value = jnp.concatenate(segments, axis=0)
    filter_grad = lax.psum_scatter(partial_value, "ctx", scatter_dimension=0, tiled=True)
    return (in_grad, filter_grad)


def table_parts(table):
    high_part = table.astype(jnp.bfloat16)
    low_part = (table - high_part.astype(np.float64)).astype(jnp.bfloat16)
    return np.stack([high_part, low_part])


def transform_tables(block):
    order = np.concatenate([np.arange(0, block, 2), np.arange(1, block, 2)])
    steps = (2 * order + 1)[:, None] * np.arange(block)[None, :] % (4 * block)
    angle = np.pi / (2 * block) * steps
    forward = np.concatenate([np.cos(angle), np.sin(angle)], axis=0)
    return table_parts(forward), table_parts(forward.T / block)


def wait_for(like, sem):
    pltpu.make_async_copy(like, like, sem).wait()


def chain_kernel(
    pair, block, chunks,
    in_ref, grad_ref, taps_ref, fwd_hbm, inv_hbm,
    out_ref, lag_ref,
    g_buf, u_buf, g_send, u_send, tap_buf, fwd, inv, g_spec, u_spec, tap_spec, sum_spec, r_high, r_low, in_buf, far_buf, in_sum, part, own_low, next_low,
    gx_sem, ux_sem, direct_sem, passed_sem, far_sem, left_u_sem, low_sem, lag_sem, out_sem, send_sem, local_sem,
    right_in, pair_in, far_in,
):
    me = lax.axis_index("ctx")
    level = lax.div(me, pair)
    side = lax.rem(me, pair)
    mate = me + 1 - 2 * side
    left, right = me - pair, me + pair
    tok_len, channels = in_ref.shape
    lag_count = taps_ref.shape[0]
    width = g_buf.shape[3]
    half = chunks * width
    segs = lag_count // block
    levels = 2 * segs
    own_lags = lag_count // (levels * pair)

    def cols(which, c):
        return pl.ds(pl.multiple_of(which * half + c * width, LANES), width)

    def rows(which, length):
        return pl.ds(pl.multiple_of(which * length, length), length)

    mine, other = rows(side, tok_len), rows(1 - side, tok_len)

    def remote(source, target, send, recv, device):
        pltpu.make_async_remote_copy(
            src_ref=source, dst_ref=target, send_sem=send, recv_sem=recv,
            device_id={"ctx": device}, device_id_type=pl.DeviceIdType.MESH,
        ).start()

    def signal(sem, device):
        pl.semaphore_signal(
            sem, inc=1, device_id={"ctx": device}, device_id_type=pl.DeviceIdType.MESH
        )

    def at_level(*which):
        hit = level == which[0]
        for value in which[1:]:
            hit = jnp.logical_or(hit, level == value)
        return pl.when(hit)

    barrier = pltpu.get_barrier_semaphore()
    signal(barrier, mate)

    @pl.when(level < levels - 1)
    def _():
        signal(barrier, right)

    every = range(chunks)
    whole = chunks // 2
    for source, kept, sent, sem in (
        (grad_ref, g_buf, g_send, local_sem.at[3]), (in_ref, u_buf, u_send, local_sem.at[4])
    ):
        for c in every:
            pltpu.make_async_copy(source.at[:, cols(1 - side, c)], sent.at[c], sem).start()
            pltpu.make_async_copy(source.at[:, cols(side, c)], kept.at[0, c, mine, :], sem).start()
    pltpu.make_async_copy(fwd_hbm, fwd, local_sem.at[0]).start()
    pltpu.make_async_copy(taps_ref.at[:, rows_of_half(side, half)], tap_buf, local_sem.at[1]).start()
    pltpu.make_async_copy(inv_hbm, inv, local_sem.at[2]).start()

    pl.semaphore_wait(barrier, 1 + jnp.minimum(level, 1))

    def mate_grads(c):
        remote(g_send.at[c], g_buf.at[0, c, mine, :], send_sem.at[0], gx_sem.at[c], mate)

    def mate_values(c):
        remote(u_send.at[c], u_buf.at[0, c, mine, :], send_sem.at[0], ux_sem.at[c], mate)

    def grads_left(c):
        remote(g_buf.at[0, c, mine, :], g_buf.at[1, c, mine, :], send_sem.at[1], direct_sem.at[c], left)

    def values_right(c):
        remote(u_buf.at[0, c, mine, :], u_buf.at[1, c, mine, :], send_sem.at[1], left_u_sem.at[c], right)

    wait_for(g_buf.at[0], local_sem.at[3])

    def forward(data, passes=FORWARD_PASSES):
        total = jnp.dot(fwd[0], data, preferred_element_type=jnp.float32)
        if passes > 1:
            total = total + jnp.dot(fwd[1], data, preferred_element_type=jnp.float32)
        return total

    def inverse(which=None):
        places = slice(None) if which is None else which
        total = jnp.dot(inv[0, places, :], r_high[...], preferred_element_type=jnp.float32)
        if INVERSE_PASSES > 1:
            total = total + jnp.dot(inv[1, places, :], r_high[...], preferred_element_type=jnp.float32)
        if INVERSE_PASSES > 2:
            total = total + jnp.dot(inv[0, places, :], r_low[...], preferred_element_type=jnp.float32)
        return total

    def over_chunks(body, split=True):
        steps = block // 2 // CHUNK
        for sign, start in ((1.0, 0), (-1.0, steps)):
            def step(index, carry, sign=sign):
                row = pl.multiple_of(index * CHUNK, CHUNK)
                re, im = pl.ds(row, CHUNK), pl.ds(row + block, CHUNK)
                spectrum = body(re, im, sign)
                for place, value in zip((re, im), spectrum if split else ()):
                    top = value.astype(jnp.bfloat16)
                    r_high[place, :] = top
                    if INVERSE_PASSES > 2:
                        r_low[place, :] = (value - top.astype(jnp.float32)).astype(jnp.bfloat16)
                return carry
            lax.fori_loop(start, start + steps, step, 0)

    def against(a, b):
        return a[0] * b[0] + a[1] * b[1], a[1] * b[0] - a[0] * b[1]

    def plus(a, b):
        return a[0] + b[0], a[1] + b[1]

    def pair_sum(grads, values, c, pairs, re, im):
        total = None
        for i, j in pairs:
            term = against(
                (grads[i, c, re, :], grads[i, c, im, :]), (values[j, c, re, :], values[j, c, im, :])
            )
            total = term if total is None else plus(total, term)
        return total

    def lags_spectrum(c, near, far):
        def body(re, im, sign):
            total = pair_sum(g_spec, u_spec, c, near, re, im)
            if far:
                real, imag = pair_sum(g_spec, u_spec, c, far, re, im)
                total = total[0] - sign * imag, total[1] + sign * real
            return total
        over_chunks(body)
        return inverse()

    def in_spectrum(c, terms, sign, re, im):
        taps = [(tap_spec[s, c, re, :], tap_spec[s, c, im, :]) for s in range(segs)]
        total = None
        for i, d in terms:
            real = imag = 0.0
            if d < segs:
                real, imag = taps[d]
            if d > 0:
                real = real + sign * taps[d - 1][1]
                imag = imag - sign * taps[d - 1][0]
            term = against((g_spec[i, c, re, :], g_spec[i, c, im, :]), (real, imag))
            total = term if total is None else plus(total, term)
        return total

    def in_terms(c, terms, summed=False):
        def body(re, im, sign):
            total = in_spectrum(c, terms, sign, re, im)
            if summed:
                total = plus(total, (sum_spec[c, re, :], sum_spec[c, im, :]))
            return total
        over_chunks(body)

    def sum_ready(c):
        def body(re, im, sign):
            sum_spec[c, re, :], sum_spec[c, im, :] = in_spectrum(c, [(0, 0), (1, 1)], sign, re, im)
        over_chunks(body, False)

    def out_place(c):
        return out_ref.at[:, cols(side, c)]

    def in_grad(c, terms, target, summed=False):
        in_terms(c, terms, summed)
        in_buf[0, c] = inverse(other).astype(jnp.bfloat16)
        remote(in_buf.at[0, c], target, send_sem.at[0], out_sem.at[0], mate)
        in_buf[1, c] = inverse(mine).astype(jnp.bfloat16)
        pltpu.make_async_copy(in_buf.at[1, c], target, out_sem.at[0]).start()

    def send_lags(c, at, owner_level, slot):
        for who in range(pair):
            owner = owner_level * pair + who
            piece = part.at[c, pl.ds(owner * own_lags, own_lags), :]
            target = lag_ref.at[slot, :, cols(side, c)]
            if owner_level != at:
                remote(piece, target, send_sem.at[2], lag_sem.at[slot], owner)
        if owner_level == at:
            def piece_of(owner):
                return part.at[c, rows(owner, own_lags), :]
            target = lag_ref.at[slot, :, cols(side, c)]
            remote(piece_of(mate), target, send_sem.at[2], lag_sem.at[slot], mate)
            pltpu.make_async_copy(piece_of(me), target, lag_sem.at[slot]).start()

    def tap_chunk(c):
        for s in range(segs):
            data = tap_buf[s * block:(s + 1) * block, c * width:(c + 1) * width]
            tap_spec[s, c] = forward(data, TAP_PASSES)

    @at_level(1, 2)
    def _():
        signal(right_in, left)

    @at_level(1, 2, 3)
    def _():
        for c in every:
            mate_grads(c)

            if c < whole:
                grads_left(c)
            else:
                @at_level(2, 3)
                def _():
                    grads_left(c)

    wait_for(u_buf.at[0], local_sem.at[4])
    for c in every:
        mate_values(c)

    @at_level(0)
    def _():
        for c in every:
            mate_grads(c)

    pltpu.make_async_copy(fwd_hbm, fwd, local_sem.at[0]).wait()
    wait_for(tap_buf, local_sem.at[1])
    tap_chunk(0)

    @at_level(0, 1)
    def _():
        pl.semaphore_wait(right_in, 1)
        for c in every:
            values_right(c)

        @at_level(0)
        def _():
            signal(pair_in, right)

    for c in every[1:]:
        tap_chunk(c)

    @at_level(1)
    def _():
        pl.semaphore_wait(pair_in, 1)
        signal(far_in, right)

    pltpu.make_async_copy(inv_hbm, inv, local_sem.at[2]).wait()

    def own_grads(c, pass_on):
        wait_for(g_buf.at[0, c, other, :], gx_sem.at[c])
        if pass_on:
            remote(g_buf.at[0, c, other, :], g_buf.at[1, c, other, :], send_sem.at[1], passed_sem.at[c], left)

    def own_values(c, pass_on):
        wait_for(u_buf.at[0, c, other, :], ux_sem.at[c])
        if pass_on:
            remote(u_buf.at[0, c, other, :], u_buf.at[1, c, other, :], send_sem.at[1], left_u_sem.at[c], right)

    def direct_grads(c, pass_on):
        wait_for(g_buf.at[1, c, mine, :], direct_sem.at[c])
        if pass_on:
            remote(g_buf.at[1, c, mine, :], g_buf.at[2, c, mine, :], send_sem.at[1], far_sem.at[c], left)

    def passed_grads(c, pass_on):
        wait_for(g_buf.at[1, c, other, :], passed_sem.at[c])
        if pass_on:
            remote(g_buf.at[1, c, other, :], g_buf.at[2, c, other, :], send_sem.at[1], far_sem.at[c], left)

    def grads_spectrum(i, c):
        g_spec[i, c] = forward(g_buf[i, c])

    def values_spectrum(i, c):
        u_spec[i, c] = forward(u_buf[i, c])

    def far_grads(c):
        wait_for(g_buf.at[2, c], far_sem.at[c])
        grads_spectrum(2, c)

    def left_values(c):
        wait_for(u_buf.at[1, c], left_u_sem.at[c])
        values_spectrum(1, c)

    low_rows, high_rows = pl.ds(0, block), pl.ds(block, block)
    low_owners = levels // 2 * pair
    turns = [
        (c, owner) for first in range(0, low_owners, pair) for c in every for owner in range(first, first + pair)
    ]

    @at_level(0)
    def _():
        for c in every:
            own_values(c, True)
            values_spectrum(0, c)
        for c in every:
            own_grads(c, False)
            grads_spectrum(0, c)
            part[c, low_rows, :] = lags_spectrum(c, [(0, 0)], []).astype(jnp.bfloat16)
            send_lags(c, 0, 0, 0)
        for c in every[whole:]:
            in_grad(c, [(0, 0)], in_sum.at[0, side, c - whole])
        for c in every[:whole]:
            direct_grads(c, False)
            passed_grads(c, False)
            grads_spectrum(1, c)
        for c in every:
            send_lags(c, 0, 1, 0)
        for c in every[:whole]:
            sum_ready(c)
            far_grads(c)
            in_grad(c, [(2, 2)], out_place(c), True)

    @at_level(1)
    def _():
        for c in every:
            own_grads(c, c < whole)
            grads_spectrum(0, c)
        for c in every:
            direct_grads(c, c < whole)
        for c in every:
            own_values(c, True)
            values_spectrum(0, c)

        def low(c):
            left_values(c)
            part[c, low_rows, :] = lags_spectrum(c, [(0, 0)], [(0, 1)]).astype(jnp.bfloat16)
            low_to(c, 0)

        def low_to(c, owner):
            piece = part.at[c, pl.ds(owner * own_lags, own_lags), :]
            remote(piece, lag_ref.at[1, :, cols(side, c)], send_sem.at[2], lag_sem.at[1], owner)

        def far_to(c, owner):
            remote(
                far_buf.at[c - whole, pl.ds(owner * tok_len, tok_len), :], in_sum.at[1, side, c - whole],
                send_sem.at[3], out_sem.at[1], owner,
            )

        def passed(c):
            passed_grads(c, c < whole)
            grads_spectrum(1, c)
            if c >= whole:
                in_terms(c, [(0, 1), (1, 2)])
                far_buf[c - whole] = inverse().astype(jnp.bfloat16)
                far_to(c, 0)

        low(0)
        for c in every[1:]:
            passed(c - 1)
            low(c)
        passed(chunks - 1)
        for owner in range(1, pair):
            for c in every[whole:]:
                far_to(c, owner)
            for c in every:
                low_to(c, owner)
        for c in every:
            send_lags(c, 1, 1, 1)
        for c in every:
            part[c, high_rows, :] = lags_spectrum(c, [(0, 1)], [(1, 1)]).astype(jnp.bfloat16)
        for c in every:
            sum_ready(c)
        for c in every:
            far_grads(c)
            if c == 0:
                for b in every:
                    send_lags(b, 1, 3, 0)
                    send_lags(b, 1, 2, 0)
            in_grad(c, [(2, 2)], out_place(c), True)

    @at_level(2)
    def _():
        lag_ref[2] = jnp.zeros(lag_ref.shape[1:], lag_ref.dtype)
        for c in every:
            own_grads(c, True)
            grads_spectrum(0, c)
            direct_grads(c, True)
        for c in every:
            own_values(c, False)
            values_spectrum(0, c)
        for c in every:
            passed_grads(c, True)
            grads_spectrum(1, c)
            left_values(c)
            own_low[c] = lags_spectrum(c, [(0, 0)], [(1, 0), (0, 1)])
        pl.semaphore_wait(far_in, 1)

        def finish_low(c, owner):
            piece = pl.ds(owner * own_lags, own_lags)
            wait_for(next_low.at[c, piece, :], low_sem.at[c, owner])
            total = own_low[c, piece, :] + next_low[c, piece, :].astype(jnp.float32)
            part[c, piece, :] = total.astype(jnp.bfloat16)
            remote(part.at[c, piece, :], lag_ref.at[2, :, cols(side, c)], send_sem.at[2], lag_sem.at[2], owner)

        def high(c):
            part[c, high_rows, :] = lags_spectrum(c, [(1, 0), (0, 1)], [(1, 1)]).astype(jnp.bfloat16)
            send_lags(c, 2, 3, 1)
            send_lags(c, 2, 2, 1)

        half_way = len(turns) // 2
        first = sorted(turns[:half_way], key=lambda turn: turn[1])
        finish_low(*first[0])
        in_grad(0, [(0, 0), (1, 1)], out_place(0))
        for turn in first[1:]:
            finish_low(*turn)
        high(0)
        for turn in turns[half_way:]:
            finish_low(*turn)
        for c in every[1:]:
            high(c)
            in_grad(c, [(0, 0), (1, 1)], out_place(c))

    @at_level(3)
    def _():
        lag_ref[2] = jnp.zeros(lag_ref.shape[1:], lag_ref.dtype)

        def next_level_low(c, owner):
            piece = pl.ds(owner * own_lags, own_lags)
            remote(part.at[c, piece, :], next_low.at[c, piece, :], send_sem.at[1], low_sem.at[c, owner], left)

        for c in every:
            own_grads(c, True)
            grads_spectrum(0, c)
        for c in every:
            own_values(c, False)
            values_spectrum(0, c)
            part[c, low_rows, :] = lags_spectrum(c, [(0, 0)], []).astype(jnp.bfloat16)
            for owner in range(pair):
                next_level_low(c, owner)
        for c, owner in turns[pair * chunks:]:
            next_level_low(c, owner)
        for c in every:
            in_grad(c, [(0, 0)], out_place(c))

    wait_for(out_ref, out_sem.at[0])

    @at_level(0)
    def _():
        wait_for(in_sum.at[1], out_sem.at[1])
        for which in range(pair):
            for c in every[whole:]:
                at = which * half + c * width
                total = in_sum[0, which, c - whole].astype(jnp.float32) + in_sum[1, which, c - whole].astype(jnp.float32)
                out_ref[:, at:at + width] = total.astype(out_ref.dtype)

    wait_for(lag_ref.at[0], lag_sem.at[0])
    wait_for(lag_ref.at[1], lag_sem.at[1])

    @at_level(0, 1)
    def _():
        wait_for(lag_ref.at[2], lag_sem.at[2])

    wait_for(g_buf.at[:, :, pl.ds(0, tok_len), :], send_sem.at[0])

    @at_level(0)
    def _():
        wait_for(g_buf.at[0], send_sem.at[1])
        wait_for(part.at[:, pl.ds(0, (levels // 2 * pair - 1) * own_lags), :], send_sem.at[2])

    @at_level(1, 2, 3)
    def _():
        wait_for(g_buf.at[pl.ds(0, 2)], send_sem.at[1])

    @at_level(1)
    def _():
        wait_for(far_buf, send_sem.at[3])

    @at_level(1, 2)
    def _():
        wait_for(part.at[:, pl.ds(0, (levels * pair - 1) * own_lags), :], send_sem.at[2])


def rows_of_half(side, half):
    return pl.ds(pl.multiple_of(side * half, LANES), half)


def finish_kernel(in_ref, lag_ref, in_out, lag_out, lag_wide, sem):
    move = pltpu.make_async_copy(in_ref, in_out, sem.at[0])
    move.start()
    wide = [lag_ref[slot].astype(lag_wide.dtype) for slot in range(lag_ref.shape[0])]
    lag_wide[...] = wide[0] + wide[1] + wide[2]
    store = pltpu.make_async_copy(lag_wide, lag_out, sem.at[1])
    store.start()
    move.wait()
    store.wait()


PAIR = 2


def chain_fits(tok_len, channels, lag_count, count):
    block = PAIR * tok_len
    return (
        count % PAIR == 0
        and lag_count == 2 * block
        and count // PAIR == 2 * (lag_count // block)
        and channels % (PAIR * CHUNKS * LANES) == 0
        and tok_len % (2 * CHUNK) == 0
        and lag_count % (count * CHUNK) == 0
    )


def per_device(inputs, out_grad, filters):
    tok_len, channels = out_grad.shape
    lag_count = filters.shape[0]
    count = lax.axis_size("ctx")
    if not chain_fits(tok_len, channels, lag_count, count):
        return general_plan(inputs, out_grad, filters)
    block = PAIR * tok_len
    segs = lag_count // block
    half = channels // PAIR
    width = half // CHUNKS
    own_lags = lag_count // count
    fwd, inv = transform_tables(block)
    bf16, f32 = jnp.bfloat16, jnp.float32
    dma = pltpu.SemaphoreType.DMA
    anywhere = pl.BlockSpec(memory_space=pl.ANY)
    in_vmem = pl.BlockSpec(memory_space=pltpu.VMEM)
    in_grad, lag_grad = pl.pallas_call(
        functools.partial(chain_kernel, PAIR, block, CHUNKS),
        out_shape=(
            pltpu.VMEM((tok_len, channels), bf16),
            pltpu.VMEM((3, own_lags, channels), bf16),
        ),
        in_specs=[anywhere] * 5,
        out_specs=(in_vmem, in_vmem),
        scratch_shapes=[
            pltpu.VMEM((3, CHUNKS, block, width), bf16),
            pltpu.VMEM((2, CHUNKS, block, width), bf16),
            pltpu.VMEM((CHUNKS, tok_len, width), bf16),
            pltpu.VMEM((CHUNKS, tok_len, width), bf16),
            pltpu.VMEM((lag_count, half), bf16),
            pltpu.VMEM(fwd.shape, bf16),
            pltpu.VMEM(inv.shape, bf16),
            pltpu.VMEM((3, CHUNKS, 2 * block, width), f32),
            pltpu.VMEM((2, CHUNKS, 2 * block, width), f32),
            pltpu.VMEM((segs, CHUNKS, 2 * block, width), f32),
            pltpu.VMEM((CHUNKS, 2 * block, width), f32),
            pltpu.VMEM((2 * block, width), bf16),
            pltpu.VMEM((2 * block, width), bf16),
            pltpu.VMEM((2, CHUNKS, tok_len, width), bf16),
            pltpu.VMEM((CHUNKS // 2, block, width), bf16),
            pltpu.VMEM((2, PAIR, CHUNKS // 2, tok_len, width), bf16),
            pltpu.VMEM((CHUNKS, lag_count, width), bf16),
            pltpu.VMEM((CHUNKS, block, width), f32),
            pltpu.VMEM((CHUNKS, block, width), bf16),
            dma((CHUNKS,)), dma((CHUNKS,)), dma((CHUNKS,)), dma((CHUNKS,)), dma((CHUNKS,)),
            dma((CHUNKS,)), dma((CHUNKS, count // 2)), dma((3,)), dma((2,)), dma((4,)), dma((5,)),
            pltpu.SemaphoreType.REGULAR,
            pltpu.SemaphoreType.REGULAR,
            pltpu.SemaphoreType.REGULAR,
        ],
        compiler_params=pltpu.CompilerParams(collective_id=0, has_side_effects=True),
    )(inputs, out_grad, filters, jnp.asarray(fwd), jnp.asarray(inv))
    return pl.pallas_call(
        finish_kernel,
        out_shape=(
            jax.ShapeDtypeStruct(in_grad.shape, bf16),
            jax.ShapeDtypeStruct(lag_grad.shape[1:], f32),
        ),
        in_specs=[in_vmem, in_vmem],
        out_specs=(anywhere, anywhere),
        scratch_shapes=[
            pltpu.VMEM(lag_grad.shape[1:], f32),
            pltpu.SemaphoreType.DMA((2,)),
        ],
    )(
        pltpu.with_memory_space_constraint(in_grad, pltpu.VMEM),
        pltpu.with_memory_space_constraint(lag_grad, pltpu.VMEM),
    )


def solution(mesh):
    return jax.shard_map(
        per_device,
        mesh=mesh,
        in_specs=(P(("groups", "ctx"), "chan"), P(("groups", "ctx"), "chan"), P(None, "chan")),
        out_specs=(P(("groups", "ctx"), "chan"), P(("groups", "ctx"), "chan")),
        check_vma=False,
    )
```
